256 devices in a mesh: pair: 32 (over y, z), state: 8 (over x, core).
Axes of the slice: x: 4, y: 4, z: 8, core: 2. Of those that a mesh axis runs over, the one named last changes fastest.
Arguments:
- states_in: float32 [128, 212992], P('state', 'pair'), may hold values from -6 to 6
- onsite: float32 [212992], P('pair'), may hold values from -1 to 1
- node_features: bfloat16 [16384, 512], P('pair', 'state'), may hold values from -6 to 6
- atom_orbitals: int32 [16384], replicated, may hold values from 4 to 13
- pair_blocks: int32 [256, 2], replicated, may hold values from 0 to 255, as said below
- pair_live: int32 [256], replicated, may hold values from 0 to 1, as said below
- weight_in: bfloat16 [512, 512], replicated, may hold values from -0.25 to 0.25
- bias_in: float32 [512], replicated, may hold values from -3 to 3
- weight_out: bfloat16 [512, 169], replicated, may hold values from -0.009765625 to 0.009765625
Outputs:
- first_step: float32 [128, 212992], P('state', 'pair')
- second_step: float32 [128, 212992], P('state', 'pair')
The draws below stay inside these ranges and needn't reach their ends.
Inputs may be any that keep to these rules, and one draw needn't show every extreme that they name: `pair_blocks`: pair slot k belongs to index k // 8 of pair, and block b to index b // 8. The two blocks of a pair differ; of the 16 blocks named by the pair slots of one index of pair, live or not, at most 1 lie on any one index, and some index holds 1 of them. `pair_live`: the live slots of each index of pair come first among its 8 slots; every index has at least one, and some index has all 8 live.
All inputs are finite; a program needn't handle non-finite values.
Results may differ from the reference program's by a relative error of at most 0.0034.
Values may be sent and summed in bfloat16 or wider, within the bound.
A program may use at most 192 MiB of HBM per device.

```python
import jax
import jax.numpy as jnp
from jax import lax

FEAT = 512
HID = 512
ORB = 13
ATOM_BLK = 64
BLK_DEV = 8
PAIR_DEV = 8
OUTW = 169
BO = 832
STATES = 128
NB = 256
ATOMS = 16384
NORB = 212992
PAIRS = 256


def pair_layout(key):
    base_key = jax.random.fold_in(key, 31)
    owner_count = NB // BLK_DEV
    end_count = 2 * PAIR_DEV
    capacity = (end_count + owner_count - 1) // owner_count
    slot_keys = jax.random.split(jax.random.fold_in(base_key, 1), owner_count)
    slot_draws = jax.vmap(lambda one_key: jax.random.permutation(one_key, owner_count * capacity)[:end_count])(slot_keys)
    owners = slot_draws // capacity
    local_index = jax.random.randint(jax.random.fold_in(base_key, 2), (owner_count, end_count), 0, BLK_DEV)
    offset = jax.random.randint(jax.random.fold_in(base_key, 3), (owner_count, PAIR_DEV), 1, BLK_DEV)
    first_owner = owners[:, 0::2]
    second_owner = owners[:, 1::2]
    first_local = local_index[:, 0::2]
    second_local = jnp.where(first_owner == second_owner, (first_local + offset) % BLK_DEV, local_index[:, 1::2])
    first_block = first_owner * BLK_DEV + first_local
    second_block = second_owner * BLK_DEV + second_local
    blocks = jnp.stack([first_block, second_block], axis=-1).reshape(owner_count * PAIR_DEV, 2).astype(jnp.int32)
    first_count = jax.random.randint(jax.random.fold_in(base_key, 4), (owner_count,), 1, PAIR_DEV + 1)
    second_count = jax.random.randint(jax.random.fold_in(base_key, 5), (owner_count,), 1, PAIR_DEV + 1)
    live_count = jnp.minimum(first_count, second_count)
    busiest = jax.random.randint(jax.random.fold_in(base_key, 6), (), 0, owner_count)
    live_count = jnp.where(jnp.arange(owner_count) == busiest, PAIR_DEV, live_count)
    live_mask = (jnp.arange(PAIR_DEV)[None, :] < live_count[:, None]).astype(jnp.int32).reshape(owner_count * PAIR_DEV)
    return (blocks, live_mask)


def draw_pair_blocks(key, part):
    return pair_layout(key)[0]


def draw_pair_live(key, part):
    return pair_layout(key)[1]


def touch_ends(drawn, own_key, low, largest):
    longest = drawn.shape.index(max(drawn.shape))
    spots = []
    for shift in (0, 1):
        where = [jax.random.randint(jax.random.fold_in(own_key, axis), (), 0, length) for axis, length in enumerate(drawn.shape)]
        where[longest] = (where[longest] + shift) % drawn.shape[longest]
        spots.append(tuple(where))
    return drawn.at[spots[0]].set(low).at[spots[1]].set(largest)


def levels(stream_key, extent, cuts, smallest, high):
    gain, own = 1.0, jax.random.fold_in(stream_key, 6)
    for dim, blocks in cuts:
        draws = jnp.exp(jax.random.uniform(jax.random.fold_in(own, dim), (blocks,), jnp.float32, smallest / len(cuts), high / len(cuts)))
        gain = gain * jnp.repeat(draws, extent[dim] // blocks).reshape([-1 if axis == dim else 1 for axis in range(len(extent))])
    return gain


def bell_draw(key, extent, spread, most, cuts=(), held_as=jnp.bfloat16):
    result = jax.random.normal(key, extent, jnp.float32) * spread
    if len(cuts) > 0:
        result = levels(key, extent, cuts, -0.22, 0.18) * result
    return jnp.clip(result, min=-most, max=most).astype(held_as)


def setup_inputs(seed: int = 0) -> dict:
    key_of = jax.random.split(jax.random.key(seed), 10)
    states_in = bell_draw(key_of[0], (STATES, NORB), 1.0, 6.0, ((0, 8), (1, 32)), jnp.float32)
    onsite = jnp.clip(jax.random.uniform(key_of[1], (NORB,), jnp.float32, -1.0, 1.0) * levels(key_of[1], (NORB,), ((0, 32),), -0.4, 0.0), -1.0, 1.0)
    node_features = bell_draw(key_of[2], (ATOMS, FEAT), 1.0, 6.0, ((0, 32), (1, 8)))
    atom_orbitals = touch_ends(jax.random.randint(key_of[3], (ATOMS,), 4, 14), jax.random.fold_in(key_of[3], 1), 4, 13).astype(jnp.int32)
    pair_blocks = draw_pair_blocks(jax.random.fold_in(key_of[9], 71), 0)
    pair_live = draw_pair_live(jax.random.fold_in(key_of[9], 71), 0)
    weight_in = bell_draw(key_of[6], (FEAT, HID), FEAT ** -0.5, 0.25)
    bias_in = bell_draw(key_of[7], (HID,), 0.5, 3.0, (), jnp.float32)
    weight_out = bell_draw(key_of[8], (HID, OUTW), (HID * BO) ** -0.5, 0.009765625)
    return {"states_in": states_in, "onsite": onsite, "node_features": node_features, "atom_orbitals": atom_orbitals, "pair_blocks": pair_blocks, "pair_live": pair_live, "weight_in": weight_in, "bias_in": bias_in, "weight_out": weight_out}


def reference(states_in, onsite, node_features, atom_orbitals, pair_blocks, pair_live, weight_in, bias_in, weight_out):
    proj_blocks = jnp.dot(node_features, weight_in, preferred_element_type=jnp.float32).reshape(NB, ATOM_BLK, HID)
    orbital_valid = (jnp.arange(ORB)[None, :] < atom_orbitals[:, None]).astype(jnp.float32).reshape(NB, BO)

    def build_tile(pair_item):
        blocks_pair, live_flag = pair_item
        first_block = blocks_pair[0].astype(jnp.int32)
        second_block = blocks_pair[1].astype(jnp.int32)

        def compute(unused):
            first_proj = lax.dynamic_index_in_dim(proj_blocks, first_block, 0, keepdims=False)
            second_proj = lax.dynamic_index_in_dim(proj_blocks, second_block, 0, keepdims=False)
            hidden = jax.nn.silu(first_proj[:, None, :] + second_proj[None, :, :] + bias_in).astype(jnp.bfloat16)
            raw_tile = jnp.dot(hidden.reshape(ATOM_BLK * ATOM_BLK, HID), weight_out, preferred_element_type=jnp.float32)
            raw_tile = raw_tile.reshape(ATOM_BLK, ATOM_BLK, ORB, ORB).transpose(0, 2, 1, 3).reshape(BO, BO)
            first_valid = lax.dynamic_index_in_dim(orbital_valid, first_block, 0, keepdims=False)
            second_valid = lax.dynamic_index_in_dim(orbital_valid, second_block, 0, keepdims=False)
            return (raw_tile * (first_valid[:, None] * second_valid[None, :])).astype(jnp.bfloat16)

        def skipped(unused):
            return jnp.zeros((BO, BO), jnp.bfloat16)

        return lax.cond(live_flag > 0, compute, skipped, 0)

    tile_set = lax.map(build_tile, (pair_blocks, pair_live))

    def operate(vector):
        def add_pair(pair_number, running):
            first_start = (pair_blocks[pair_number, 0] * BO).astype(jnp.int32)
            second_start = (pair_blocks[pair_number, 1] * BO).astype(jnp.int32)

            def touch(current):
                tile_wide = tile_set[pair_number].astype(jnp.float32)
                first_field = lax.dynamic_slice_in_dim(vector, first_start, BO, 1)
                second_field = lax.dynamic_slice_in_dim(vector, second_start, BO, 1)
                first_sum = lax.dynamic_slice_in_dim(current, first_start, BO, 1) + lax.dot_general(
                    second_field, tile_wide, (((1,), (1,)), ((), ())), precision=lax.Precision.HIGHEST)
                current = lax.dynamic_update_slice_in_dim(current, first_sum, first_start, 1)
                second_sum = lax.dynamic_slice_in_dim(current, second_start, BO, 1) + jnp.dot(
                    first_field, tile_wide, precision=lax.Precision.HIGHEST)
                return lax.dynamic_update_slice_in_dim(current, second_sum, second_start, 1)

            return lax.cond(pair_live[pair_number] > 0, touch, lambda current: current, running)

        return lax.fori_loop(0, PAIRS, add_pair, vector * onsite[None, :])

    first_step = operate(states_in)
    second_step = 2.0 * operate(first_step) - states_in
    return first_step, second_step
```

```python
import functools

import jax
import jax.numpy as jnp
from jax import lax
from jax.experimental import pallas as pl
from jax.experimental.pallas import tpu as pltpu
from jax.sharding import PartitionSpec as P

ORB = 13
ATOM_BLK = 64
BO = 832
HALF = ATOM_BLK // 2
OUTP = 176
BOP = 896
MESH = pl.DeviceIdType.MESH
BF = jnp.bfloat16
F32 = jnp.float32
NT = (((1,), (1,)), ((), ()))


def kernel(
    np_, ns_, tab, wv, orb, vst, on, feat, w_in, bias, w_out, o1, o2,
    fp, fsend, frecv, fx, fxr, proj, s2, t1, tile, vb, gsend, grecv, xs, xr, ys, yr, rsend, rrecv,
    psend, precv, ssend, srecv,
):
    me_p = lax.axis_index("pair")
    me_s = lax.axis_index("state")
    rows = vst.shape[1]
    blocks = vst.shape[0]
    inv_at, slot_at = np_, 2 * np_

    barrier = pltpu.get_barrier_semaphore()

    def greet_pair(i, c):
        pl.semaphore_signal(
            barrier, inc=1, device_id=(lax.rem(me_p + i, np_), me_s), device_id_type=MESH
        )
        return c

    def greet_state(i, c):
        pl.semaphore_signal(
            barrier, inc=1, device_id=(me_p, lax.rem(me_s + i, ns_)), device_id_type=MESH
        )
        return c

    lax.fori_loop(1, np_, greet_pair, 0)
    lax.fori_loop(1, ns_, greet_state, 0)

    def pair_copy(phase, src, dst, slot_src, slot_dst, dev):
        return pltpu.make_async_remote_copy(
            src_ref=src.at[slot_src],
            dst_ref=dst.at[slot_dst],
            send_sem=psend.at[phase, slot_src],
            recv_sem=precv.at[phase, slot_dst],
            device_id=(dev, me_s),
            device_id_type=MESH,
        )

    def pair_start(phase, src, dst):
        def go(i, c):
            d = lax.rem(me_p + i, np_)
            pair_copy(phase, src, dst, d, me_p, d).start()
            return c

        lax.fori_loop(1, np_, go, 0)

    def pair_wait(phase, src, dst):
        def go(i, c):
            d = lax.rem(me_p + np_ - i, np_)
            pair_copy(phase, src, dst, d, d, d).wait_recv()
            return c

        lax.fori_loop(1, np_, go, 0)

    def pair_drain(phase, src, dst):
        def go(i, c):
            d = lax.rem(me_p + i, np_)
            pair_copy(phase, src, dst, d, me_p, d).wait_send()
            return c

        lax.fori_loop(1, np_, go, 0)

    def state_copy(phase, src, dst, slot_src, slot_dst, dev):
        return pltpu.make_async_remote_copy(
            src_ref=src.at[slot_src],
            dst_ref=dst.at[slot_dst],
            send_sem=ssend.at[phase, slot_src],
            recv_sem=srecv.at[phase, slot_dst],
            device_id=(me_p, dev),
            device_id_type=MESH,
        )

    def state_start(phase, src, dst):
        def go(i, c):
            d = lax.rem(me_s + i, ns_)
            state_copy(phase, src, dst, d, me_s, d).start()
            return c

        lax.fori_loop(1, ns_, go, 0)

    def state_wait(phase, src, dst):
        def go(i, c):
            d = lax.rem(me_s + ns_ - i, ns_)
            state_copy(phase, src, dst, d, d, d).wait_recv()
            return c

        lax.fori_loop(1, ns_, go, 0)

    def state_drain(phase, src, dst):
        def go(i, c):
            d = lax.rem(me_s + i, ns_)
            state_copy(phase, src, dst, d, me_s, d).wait_send()
            return c

        lax.fori_loop(1, ns_, go, 0)

    for b in range(blocks):
        low = feat[b * ATOM_BLK : b * ATOM_BLK + HALF, :]
        high = feat[b * ATOM_BLK + HALF : (b + 1) * ATOM_BLK, :]
        fp[b] = jnp.concatenate([low, high], axis=1)
        vb[0, b] = vst[b].astype(BF)

    def fill(d, c):
        pick = tab[d]
        fsend[d] = fp[pick]
        gsend[0, d] = vb[0, pick]
        return c

    lax.fori_loop(0, np_, fill, 0)
    frecv[me_p] = fp[tab[me_p]]
    grecv[0, me_p] = vb[0, tab[me_p]]

    pl.semaphore_wait(barrier, np_ + ns_ - 2)
    pair_start(0, fsend, frecv)
    pair_start(1, gsend.at[0], grecv.at[0])

    lane = lax.broadcasted_iota(jnp.int32, (HALF, 2 * ATOM_BLK), 1)
    right_half = lane >= ATOM_BLK
    row_atom = 2 * lax.broadcasted_iota(jnp.int32, (HALF, ATOM_BLK), 0)
    col_atom = lax.broadcasted_iota(jnp.int32, (HALF, ATOM_BLK), 1)
    orb_i, orb_j = orb[0:1, :], orb[1:2, :]
    even = jnp.sum(jnp.where(col_atom == row_atom, orb_i, 0), axis=1, keepdims=True)
    odd = jnp.sum(jnp.where(col_atom == row_atom + 1, orb_i, 0), axis=1, keepdims=True)
    valid_i = jnp.where(right_half, odd, even)
    valid_j = jnp.concatenate(
        [jnp.broadcast_to(orb_j, (HALF, ATOM_BLK)), jnp.broadcast_to(orb_j, (HALF, ATOM_BLK))], axis=1
    )

    pair_wait(0, fsend, frecv)

    def fill_fx(k, c):
        fx[k, 0] = frecv[tab[slot_at + 2 * k]]
        fx[k, 1] = frecv[tab[slot_at + 2 * k + 1]]
        return c

    lax.fori_loop(0, ns_, fill_fx, 0)
    fxr[me_s] = fx[me_s]
    state_start(0, fx, fxr)
    state_wait(0, fx, fxr)

    parts = []
    for side in range(2):
        for half in range(2):
            parts.append(
                jnp.concatenate(
                    [
                        fxr[s, side][:, half * ATOM_BLK : (half + 1) * ATOM_BLK]
                        for s in range(ns_)
                    ],
                    axis=1,
                )
            )
    both = jnp.concatenate(parts, axis=0)
    proj[...] = jnp.dot(both, w_in[...], preferred_element_type=F32)
    proj[0:ATOM_BLK, :] = proj[0:ATOM_BLK, :] + bias[...]

    def hidden_step(c, carry):
        second = proj[ATOM_BLK : 2 * ATOM_BLK, :]
        pieces = []
        for t in range(4):
            half_v = 0.5 * (proj[pl.ds(4 * c + t, 1), :] + second)
            pieces.append((half_v + half_v * jnp.tanh(half_v)).astype(BF))
        hidden = jnp.concatenate(pieces, axis=0)
        out = lax.dot_general(w_out[...], hidden, NT, preferred_element_type=F32)
        start = pl.multiple_of(2 * c * OUTP, 8)
        s2[pl.ds(start, OUTP), :] = out[:, 0 : 2 * ATOM_BLK]
        s2[pl.ds(start + OUTP, OUTP), :] = out[:, 2 * ATOM_BLK : 4 * ATOM_BLK]
        return carry

    lax.fori_loop(0, ATOM_BLK // 4, hidden_step, 0)

    def orbital_step(p, carry):
        row_ok = valid_i > p
        for q in range(0, ORB, 2):
            first = jnp.where(
                row_ok & (valid_j > q), s2[pl.ds(p * ORB + q, HALF, stride=OUTP), :], 0.0
            )
            if q + 1 < ORB:
                second = jnp.where(
                    row_ok & (valid_j > q + 1),
                    s2[pl.ds(p * ORB + q + 1, HALF, stride=OUTP), :],
                    0.0,
                )
            else:
                second = jnp.zeros_like(first)
            at = (q // 2) * BO
            t1[pl.ds(at + p, HALF, stride=2 * ORB), :] = jnp.where(
                right_half, pltpu.roll(second, ATOM_BLK, 1), first
            )
            t1[pl.ds(at + p + ORB, HALF, stride=2 * ORB), :] = jnp.where(
                right_half, second, pltpu.roll(first, ATOM_BLK, 1)
            )
        return carry

    lax.fori_loop(0, ORB, orbital_step, 0)

    source = lax.broadcasted_iota(jnp.int32, (BOP, 1), 0)
    target = lax.rem(source, ATOM_BLK) * ORB + source // ATOM_BLK
    target = jnp.where(source < BO, target, -1)
    step_rows = BO // 2
    for n in range(0, BO, 256):
        width = min(256, BO - n)
        move = (target == n + lax.broadcasted_iota(jnp.int32, (BOP, width), 1)).astype(F32).astype(BF)
        for r in range(0, BO, step_rows):
            strip = jnp.concatenate(
                [t1[g * BO + r : g * BO + r + step_rows, :].astype(BF) for g in range(BOP // 128)], axis=1
            )
            tile[r : r + step_rows, n : n + width] = jnp.dot(
                strip, move, preferred_element_type=F32
            ).astype(BF)

    slots = np_ * rows
    out_rows = blocks * rows
    row_id = lax.broadcasted_iota(jnp.int32, (out_rows, slots), 0)
    col_id = lax.broadcasted_iota(jnp.int32, (out_rows, slots), 1)
    collect = (
        (wv[...] == row_id // rows) & (lax.rem(row_id, rows) == lax.rem(col_id, rows))
    ).astype(F32).astype(BF)

    def apply(step):
        gs, gr, rs, rr = gsend.at[step], grecv.at[step], rsend.at[step], rrecv.at[step]
        pair_wait(1 + 2 * step, gs, gr)

        def fill_x(k, c):
            xs[step, k, 0] = gr[tab[slot_at + 2 * k]]
            xs[step, k, 1] = gr[tab[slot_at + 2 * k + 1]]
            return c

        lax.fori_loop(0, ns_, fill_x, 0)
        xr[step, me_s] = xs[step, me_s]
        state_start(1 + 2 * step, xs.at[step], xr.at[step])
        state_wait(1 + 2 * step, xs.at[step], xr.at[step])
        field_i = xr[step, :, 0].reshape(ns_ * rows, BO)
        field_j = xr[step, :, 1].reshape(ns_ * rows, BO)
        to_first = lax.dot_general(field_j, tile[...], NT, preferred_element_type=F32)
        to_second = jnp.dot(field_i, tile[...], preferred_element_type=F32)
        ys[step, :, 0] = to_first.astype(BF).reshape(ns_, rows, BO)
        ys[step, :, 1] = to_second.astype(BF).reshape(ns_, rows, BO)
        yr[step, me_s] = ys[step, me_s]
        state_start(2 + 2 * step, ys.at[step], yr.at[step])
        state_wait(2 + 2 * step, ys.at[step], yr.at[step])

        def fill_r(p, c):
            e = tab[inv_at + p]
            rs[p] = yr[step, e // 2, lax.rem(e, 2)]
            return c

        lax.fori_loop(0, np_, fill_r, 0)
        mine = tab[inv_at + me_p]
        rr[me_p] = yr[step, mine // 2, lax.rem(mine, 2)]
        pair_start(2 + 2 * step, rs, rr)
        pair_wait(2 + 2 * step, rs, rr)
        sums = jnp.dot(collect, rr[...].reshape(slots, BO), preferred_element_type=F32)
        return sums.reshape(blocks, rows, BO)

    first = vst[...] * on[...] + apply(0)
    o1[...] = first
    vb[1] = first.astype(BF)

    def fill_again(d, c):
        gsend[1, d] = vb[1, tab[d]]
        return c

    lax.fori_loop(0, np_, fill_again, 0)
    grecv[1, me_p] = vb[1, tab[me_p]]
    pair_start(3, gsend.at[1], grecv.at[1])
    o2[...] = 2.0 * (o1[...] * on[...] + apply(1)) - vst[...]

    pair_drain(0, fsend, frecv)
    state_drain(0, fx, fxr)
    for step in range(2):
        pair_drain(1 + 2 * step, gsend.at[step], grecv.at[step])
        pair_drain(2 + 2 * step, rsend.at[step], rrecv.at[step])
        state_drain(1 + 2 * step, xs.at[step], xr.at[step])
        state_drain(2 + 2 * step, ys.at[step], yr.at[step])


def per_device(
    states_in, onsite, node_features, atom_orbitals, pair_blocks, pair_live, weight_in, bias_in, weight_out
):
    np_ = lax.axis_size("pair")
    ns_ = lax.axis_size("state")
    me_p = lax.axis_index("pair")
    me_s = lax.axis_index("state")
    rows = states_in.shape[0]
    blocks = onsite.shape[0] // BO
    pairs_here = pair_blocks.shape[0] // np_
    ends = 2 * pairs_here
    table = pair_blocks.reshape(np_, ends)
    owner, local = table // blocks, table % blocks
    want = jnp.max(jnp.where(owner == me_p, local, -1), axis=1)
    my_ends = lax.dynamic_index_in_dim(table, me_p, 0, keepdims=False)
    my_owner = my_ends // blocks
    hit = my_owner[None, :] == jnp.arange(np_)[:, None]
    inverse = jnp.max(jnp.where(hit, jnp.arange(ends)[None, :], 0), axis=1)
    tab = jnp.concatenate([jnp.maximum(want, 0), inverse, my_owner]).astype(jnp.int32)
    wv = jnp.repeat(want, rows)[None, :].astype(jnp.int32)
    my_pair = lax.dynamic_index_in_dim(pair_blocks, me_p * pairs_here + me_s, 0, keepdims=False)
    live = lax.dynamic_index_in_dim(pair_live, me_p * pairs_here + me_s, 0, keepdims=False)
    orb = jnp.take(atom_orbitals.reshape(-1, ATOM_BLK), my_pair, axis=0) * (live > 0).astype(jnp.int32)
    vst = states_in.reshape(rows, blocks, BO).transpose(1, 0, 2)
    w_out = jnp.pad(weight_out.T, ((0, OUTP - ORB * ORB), (0, 0)))
    hid = weight_in.shape[1]
    block = (rows, BO)
    vmem = pl.BlockSpec(memory_space=pltpu.VMEM)
    out = jax.ShapeDtypeStruct((blocks,) + block, F32)
    packed = (HALF, 2 * ATOM_BLK)
    o1, o2 = pl.pallas_call(
        functools.partial(kernel, np_, ns_),
        out_shape=(out, out),
        in_specs=[pl.BlockSpec(memory_space=pltpu.SMEM)] + [vmem] * 8,
        out_specs=(vmem, vmem),
        scratch_shapes=[
            pltpu.VMEM((blocks,) + packed, BF),
            pltpu.VMEM((np_,) + packed, BF),
            pltpu.VMEM((np_,) + packed, BF),
            pltpu.VMEM((ns_, 2) + packed, BF),
            pltpu.VMEM((ns_, 2) + packed, BF),
            pltpu.VMEM((2 * ATOM_BLK, hid), F32),
            pltpu.VMEM((HALF * OUTP, 2 * ATOM_BLK), F32),
            pltpu.VMEM((BO * BOP // 128, 128), F32),
            pltpu.VMEM((BO, BO), BF),
            pltpu.VMEM((2, blocks) + block, BF),
            pltpu.VMEM((2, np_) + block, BF),
            pltpu.VMEM((2, np_) + block, BF),
            pltpu.VMEM((2, ns_, 2) + block, BF),
            pltpu.VMEM((2, ns_, 2) + block, BF),
            pltpu.VMEM((2, ns_, 2) + block, BF),
            pltpu.VMEM((2, ns_, 2) + block, BF),
            pltpu.VMEM((2, np_) + block, BF),
            pltpu.VMEM((2, np_) + block, BF),
            pltpu.SemaphoreType.DMA((5, np_)),
            pltpu.SemaphoreType.DMA((5, np_)),
            pltpu.SemaphoreType.DMA((5, ns_)),
            pltpu.SemaphoreType.DMA((5, ns_)),
        ],
        compiler_params=pltpu.CompilerParams(collective_id=0, has_side_effects=True, vmem_limit_bytes=60 << 20),
        name="chebyshev",
    )(tab, wv, orb, vst, onsite.reshape(blocks, 1, BO), node_features, weight_in, bias_in[None, :], w_out)
    return tuple(o.transpose(1, 0, 2).reshape(rows, blocks * BO) for o in (o1, o2))


def solution(mesh):
    return jax.shard_map(
        per_device,
        mesh=mesh,
        in_specs=(P("state", "pair"), P("pair"), P("pair", "state"), P(), P(), P(), P(), P(), P()),
        out_specs=(P("state", "pair"), P("state", "pair")),
        check_vma=False,
    )
```

```python
import functools

import jax
import jax.numpy as jnp
from jax import lax
from jax.experimental import pallas as pl
from jax.experimental.pallas import tpu as pltpu
from jax.sharding import PartitionSpec as P

ORB = 13
ATOM_BLK = 64
BO = 832
HALF = ATOM_BLK // 2
OUTP = 176
BOP = 896
MESH = pl.DeviceIdType.MESH
BF = jnp.bfloat16
F32 = jnp.float32
NT = (((1,), (1,)), ((), ()))


def kernel(
    np_, ns_, tab, wv, orb, vst, on, feat, w_in, bias, w_out, o1, o2,
    fp, fsend, frecv, fx, fxr, proj, s2, t1, tile, vb, gsend, xs, xr, ys, rsend, rrecv,
    psend, precv, ssend, srecv, *split,
):
    me_p = lax.axis_index("pair")
    me_s = lax.axis_index("state")
    rows = vst.shape[1] // 2
    blocks = vst.shape[0]
    inv_at, slot_at = np_, 2 * np_
    grecv, yr = split[:4], split[4:]

    barrier = pltpu.get_barrier_semaphore()

    def greet_pair(i, c):
        pl.semaphore_signal(
            barrier, inc=1, device_id=(lax.rem(me_p + i, np_), me_s), device_id_type=MESH
        )
        return c

    def greet_state(i, c):
        pl.semaphore_signal(
            barrier, inc=1, device_id=(me_p, lax.rem(me_s + i, ns_)), device_id_type=MESH
        )
        return c

    lax.fori_loop(1, np_, greet_pair, 0)
    lax.fori_loop(1, ns_, greet_state, 0)

    def pair_copy(phase, src, dst, slot_src, slot_dst, dev):
        return pltpu.make_async_remote_copy(
            src_ref=src.at[slot_src],
            dst_ref=dst.at[slot_dst],
            send_sem=psend.at[phase, slot_src],
            recv_sem=precv.at[phase, slot_dst],
            device_id=(dev, me_s),
            device_id_type=MESH,
        )

    def pair_start(phase, src, dst):
        def go(i, c):
            d = lax.rem(me_p + i, np_)
            pair_copy(phase, src, dst, d, me_p, d).start()
            return c

        lax.fori_loop(1, np_, go, 0)

    def pair_wait(phase, src, dst):
        def go(i, c):
            d = lax.rem(me_p + np_ - i, np_)
            pair_copy(phase, src, dst, d, d, d).wait_recv()
            return c

        lax.fori_loop(1, np_, go, 0)

    def pair_drain(phase, src, dst):
        def go(i, c):
            d = lax.rem(me_p + i, np_)
            pair_copy(phase, src, dst, d, me_p, d).wait_send()
            return c

        lax.fori_loop(1, np_, go, 0)

    def state_copy(phase, src, dst, slot_src, slot_dst, dev):
        return pltpu.make_async_remote_copy(
            src_ref=src.at[slot_src],
            dst_ref=dst.at[slot_dst],
            send_sem=ssend.at[phase, slot_src],
            recv_sem=srecv.at[phase, slot_dst],
            device_id=(me_p, dev),
            device_id_type=MESH,
        )

    def state_start(phase, src, dst):
        def go(i, c):
            d = lax.rem(me_s + i, ns_)
            state_copy(phase, src, dst, d, me_s, d).start()
            return c

        lax.fori_loop(1, ns_, go, 0)

    def state_wait(phase, src, dst):
        def go(i, c):
            d = lax.rem(me_s + ns_ - i, ns_)
            state_copy(phase, src, dst, d, d, d).wait_recv()
            return c

        lax.fori_loop(1, ns_, go, 0)

    def state_drain(phase, src, dst):
        def go(i, c):
            d = lax.rem(me_s + i, ns_)
            state_copy(phase, src, dst, d, me_s, d).wait_send()
            return c

        lax.fori_loop(1, ns_, go, 0)

    for b in range(blocks):
        low = feat[b * ATOM_BLK : b * ATOM_BLK + HALF, :]
        high = feat[b * ATOM_BLK + HALF : (b + 1) * ATOM_BLK, :]
        fp[b] = jnp.concatenate([low, high], axis=1)
        for h in range(2):
            vb[h, b] = vst[b, h * rows : (h + 1) * rows, :].astype(BF)

    def fill(d, c):
        pick = tab[d]
        fsend[d] = fp[pick]
        for h in range(2):
            gsend[h, d] = vb[h, pick]
        return c

    lax.fori_loop(0, np_, fill, 0)
    frecv[me_p] = fp[tab[me_p]]
    for h in range(2):
        grecv[h][me_p] = vb[h, tab[me_p]]

    pl.semaphore_wait(barrier, np_ + ns_ - 2)
    pair_start(0, fsend, frecv)
    for h in range(2):
        pair_start(1 + h, gsend.at[h], grecv[h])

    lane = lax.broadcasted_iota(jnp.int32, (HALF, 2 * ATOM_BLK), 1)
    right_half = lane >= ATOM_BLK
    row_atom = 2 * lax.broadcasted_iota(jnp.int32, (HALF, ATOM_BLK), 0)
    col_atom = lax.broadcasted_iota(jnp.int32, (HALF, ATOM_BLK), 1)
    orb_i, orb_j = orb[0:1, :], orb[1:2, :]
    even = jnp.sum(jnp.where(col_atom == row_atom, orb_i, 0), axis=1, keepdims=True)
    odd = jnp.sum(jnp.where(col_atom == row_atom + 1, orb_i, 0), axis=1, keepdims=True)
    valid_i = jnp.where(right_half, odd, even)
    valid_j = jnp.concatenate(
        [jnp.broadcast_to(orb_j, (HALF, ATOM_BLK)), jnp.broadcast_to(orb_j, (HALF, ATOM_BLK))], axis=1
    )

    pair_wait(0, fsend, frecv)

    def fill_fx(k, c):
        fx[k, 0] = frecv[tab[slot_at + 2 * k]]
        fx[k, 1] = frecv[tab[slot_at + 2 * k + 1]]
        return c

    lax.fori_loop(0, ns_, fill_fx, 0)
    fxr[me_s] = fx[me_s]
    state_start(0, fx, fxr)
    state_wait(0, fx, fxr)

    parts = []
    for side in range(2):
        for half in range(2):
            parts.append(
                jnp.concatenate(
                    [
                        fxr[s, side][:, half * ATOM_BLK : (half + 1) * ATOM_BLK]
                        for s in range(ns_)
                    ],
                    axis=1,
                )
            )
    both = jnp.concatenate(parts, axis=0)
    proj[...] = jnp.dot(both, w_in[...], preferred_element_type=F32)
    proj[0:ATOM_BLK, :] = proj[0:ATOM_BLK, :] + bias[...]

    def hidden_step(c, carry):
        second = proj[ATOM_BLK : 2 * ATOM_BLK, :]
        pieces = []
        for t in range(4):
            half_v = 0.5 * (proj[pl.ds(4 * c + t, 1), :] + second)
            pieces.append((half_v + half_v * jnp.tanh(half_v)).astype(BF))
        hidden = jnp.concatenate(pieces, axis=0)
        out = lax.dot_general(w_out[...], hidden, NT, preferred_element_type=F32)
        start = pl.multiple_of(2 * c * OUTP, 8)
        s2[pl.ds(start, OUTP), :] = out[:, 0 : 2 * ATOM_BLK]
        s2[pl.ds(start + OUTP, OUTP), :] = out[:, 2 * ATOM_BLK : 4 * ATOM_BLK]
        return carry

    lax.fori_loop(0, ATOM_BLK // 4, hidden_step, 0)

    def orbital_step(p, carry):
        row_ok = valid_i > p
        for q in range(0, ORB, 2):
            first = jnp.where(
                row_ok & (valid_j > q), s2[pl.ds(p * ORB + q, HALF, stride=OUTP), :], 0.0
            )
            if q + 1 < ORB:
                second = jnp.where(
                    row_ok & (valid_j > q + 1),
                    s2[pl.ds(p * ORB + q + 1, HALF, stride=OUTP), :],
                    0.0,
                )
            else:
                second = jnp.zeros_like(first)
            at = (q // 2) * BO
            t1[pl.ds(at + p, HALF, stride=2 * ORB), :] = jnp.where(
                right_half, pltpu.roll(second, ATOM_BLK, 1), first
            )
            t1[pl.ds(at + p + ORB, HALF, stride=2 * ORB), :] = jnp.where(
                right_half, second, pltpu.roll(first, ATOM_BLK, 1)
            )
        return carry

    slots = np_ * rows
    out_rows = blocks * rows
    row_id = lax.broadcasted_iota(jnp.int32, (out_rows, slots), 0)
    col_id = lax.broadcasted_iota(jnp.int32, (out_rows, slots), 1)
    collect = (
        (wv[...] == row_id // rows) & (lax.rem(row_id, rows) == lax.rem(col_id, rows))
    ).astype(F32).astype(BF)

    def take_fields(job):
        gs, gr = gsend.at[job], grecv[job]
        pair_wait(1 + job, gs, gr)

        def fill_x(k, c):
            xs[job, k, 0] = gr[tab[slot_at + 2 * k]]
            xs[job, k, 1] = gr[tab[slot_at + 2 * k + 1]]
            return c

        lax.fori_loop(0, ns_, fill_x, 0)
        xr[job, me_s] = xs[job, me_s]
        state_start(1 + job, xs.at[job], xr.at[job])

    def multiply(job):
        state_wait(1 + job, xs.at[job], xr.at[job])
        fields = xr[job].astype(F32)
        field_i = fields[:, 0].reshape(ns_ * rows, BO).astype(BF)
        field_j = fields[:, 1].reshape(ns_ * rows, BO).astype(BF)
        to_first = lax.dot_general(field_j, tile[...], NT, preferred_element_type=F32)
        to_second = jnp.dot(field_i, tile[...], preferred_element_type=F32)
        ys[job, :, 0] = to_first.reshape(ns_, rows, BO).astype(BF)
        ys[job, :, 1] = to_second.reshape(ns_, rows, BO).astype(BF)
        yr[job][me_s] = ys[job, me_s]
        state_start(5 + job, ys.at[job], yr[job])

    def give_back(job):
        state_wait(5 + job, ys.at[job], yr[job])

        def fill_r(p, c):
            e = tab[inv_at + p]
            rsend[job, p] = yr[job][e // 2, lax.rem(e, 2)]
            return c

        lax.fori_loop(0, np_, fill_r, 0)
        mine = tab[inv_at + me_p]
        rrecv[job, me_p] = yr[job][mine // 2, lax.rem(mine, 2)]
        pair_start(5 + job, rsend.at[job], rrecv.at[job])

    def collect_sums(job):
        pair_wait(5 + job, rsend.at[job], rrecv.at[job])
        arrived = rrecv[job].astype(F32).reshape(slots, BO).astype(BF)
        sums = jnp.dot(collect, arrived, preferred_element_type=F32)
        return sums.reshape(blocks, rows, BO)

    def update(h):
        part = slice(h * rows, (h + 1) * rows)
        first = vst[:, part, :] * on[...] + collect_sums(h)
        o1[:, part, :] = first
        vb[2 + h] = first.astype(BF)

        def fill_again(d, c):
            gsend[2 + h, d] = vb[2 + h, tab[d]]
            return c

        lax.fori_loop(0, np_, fill_again, 0)
        grecv[2 + h][me_p] = vb[2 + h, tab[me_p]]
        pair_start(3 + h, gsend.at[2 + h], grecv[2 + h])

    def finish(h):
        part = slice(h * rows, (h + 1) * rows)
        o2[:, part, :] = 2.0 * (o1[:, part, :] * on[...] + collect_sums(2 + h)) - vst[:, part, :]

    take_fields(0)
    lax.fori_loop(0, ORB, orbital_step, 0)

    source = lax.broadcasted_iota(jnp.int32, (BOP, 1), 0)
    target = lax.rem(source, ATOM_BLK) * ORB + source // ATOM_BLK
    target = jnp.where(source < BO, target, -1)
    step_rows = BO // 2
    for n in range(0, BO, 256):
        width = min(256, BO - n)
        move = (target == n + lax.broadcasted_iota(jnp.int32, (BOP, width), 1)).astype(F32).astype(BF)
        for r in range(0, BO, step_rows):
            strip = jnp.concatenate(
                [t1[g * BO + r : g * BO + r + step_rows, :].astype(BF) for g in range(BOP // 128)], axis=1
            )
            tile[r : r + step_rows, n : n + width] = jnp.dot(
                strip, move, preferred_element_type=F32
            ).astype(BF)
    for step in range(2):
        first_job, second_job = 2 * step, 2 * step + 1
        if step == 1:
            take_fields(first_job)
        multiply(first_job)
        take_fields(second_job)
        give_back(first_job)
        multiply(second_job)
        give_back(second_job)
        for h in range(2):
            (finish if step else update)(h)

    pair_drain(0, fsend, frecv)
    state_drain(0, fx, fxr)
    for job in range(4):
        pair_drain(1 + job, gsend.at[job], grecv[job])
        pair_drain(5 + job, rsend.at[job], rrecv.at[job])
        state_drain(1 + job, xs.at[job], xr.at[job])
        state_drain(5 + job, ys.at[job], yr[job])


def per_device(
    states_in, onsite, node_features, atom_orbitals, pair_blocks, pair_live, weight_in, bias_in, weight_out
):
    np_ = lax.axis_size("pair")
    ns_ = lax.axis_size("state")
    me_p = lax.axis_index("pair")
    me_s = lax.axis_index("state")
    rows = states_in.shape[0]
    blocks = onsite.shape[0] // BO
    pairs_here = pair_blocks.shape[0] // np_
    ends = 2 * pairs_here
    table = pair_blocks.reshape(np_, ends)
    owner, local = table // blocks, table % blocks
    want = jnp.max(jnp.where(owner == me_p, local, -1), axis=1)
    my_ends = lax.dynamic_index_in_dim(table, me_p, 0, keepdims=False)
    my_owner = my_ends // blocks
    hit = my_owner[None, :] == jnp.arange(np_)[:, None]
    inverse = jnp.max(jnp.where(hit, jnp.arange(ends)[None, :], 0), axis=1)
    tab = jnp.concatenate([jnp.maximum(want, 0), inverse, my_owner]).astype(jnp.int32)
    wv = jnp.repeat(want, rows // 2)[None, :].astype(jnp.int32)
    my_pair = lax.dynamic_index_in_dim(pair_blocks, me_p * pairs_here + me_s, 0, keepdims=False)
    live = lax.dynamic_index_in_dim(pair_live, me_p * pairs_here + me_s, 0, keepdims=False)
    orb = jnp.take(atom_orbitals.reshape(-1, ATOM_BLK), my_pair, axis=0) * (live > 0).astype(jnp.int32)
    vst = states_in.reshape(rows, blocks, BO).transpose(1, 0, 2)
    w_out = jnp.pad(weight_out.T, ((0, OUTP - ORB * ORB), (0, 0)))
    hid = weight_in.shape[1]
    block, part = (rows, BO), (rows // 2, BO)
    vmem = pl.BlockSpec(memory_space=pltpu.VMEM)
    out = jax.ShapeDtypeStruct((blocks,) + block, F32)
    packed = (HALF, 2 * ATOM_BLK)
    o1, o2 = pl.pallas_call(
        functools.partial(kernel, np_, ns_),
        out_shape=(out, out),
        in_specs=[pl.BlockSpec(memory_space=pltpu.SMEM)] + [vmem] * 8,
        out_specs=(vmem, vmem),
        scratch_shapes=[
            pltpu.VMEM((blocks,) + packed, BF),
            pltpu.VMEM((np_,) + packed, BF),
            pltpu.VMEM((np_,) + packed, BF),
            pltpu.VMEM((ns_, 2) + packed, BF),
            pltpu.VMEM((ns_, 2) + packed, BF),
            pltpu.VMEM((2 * ATOM_BLK, hid), F32),
            pltpu.VMEM((HALF * OUTP, 2 * ATOM_BLK), F32),
            pltpu.VMEM((BO * BOP // 128, 128), F32),
            pltpu.VMEM((BO, BO), BF),
            pltpu.VMEM((4, blocks) + part, BF),
            pltpu.VMEM((4, np_) + part, BF),
            pltpu.VMEM((4, ns_, 2) + part, BF),
            pltpu.VMEM((4, ns_, 2) + part, BF),
            pltpu.VMEM((4, ns_, 2) + part, BF),
            pltpu.VMEM((4, np_) + part, BF),
            pltpu.VMEM((4, np_) + part, BF),
            pltpu.SemaphoreType.DMA((9, np_)),
            pltpu.SemaphoreType.DMA((9, np_)),
            pltpu.SemaphoreType.DMA((9, ns_)),
            pltpu.SemaphoreType.DMA((9, ns_)),
        ]
        + [pltpu.VMEM((np_,) + part, BF)] * 4
        + [pltpu.VMEM((ns_, 2) + part, BF)] * 4,
        compiler_params=pltpu.CompilerParams(collective_id=0, has_side_effects=True, vmem_limit_bytes=60 << 20),
        name="chebyshev",
    )(tab, wv, orb, vst, onsite.reshape(blocks, 1, BO), node_features, weight_in, bias_in[None, :], w_out)
    return tuple(o.transpose(1, 0, 2).reshape(rows, blocks * BO) for o in (o1, o2))


def solution(mesh):
    return jax.shard_map(
        per_device,
        mesh=mesh,
        in_specs=(P("state", "pair"), P("pair"), P("pair", "state"), P(), P(), P(), P(), P(), P()),
        out_specs=(P("state", "pair"), P("state", "pair")),
        check_vma=False,
    )
```
